256 devices in a mesh: row: 8 (over y, x_lo), col: 32 (over z, x_hi, core).
Axes of the slice: x: 4 (x_hi: 2, x_lo: 2; x = x_hi * 2 + x_lo), y: 4, z: 8, core: 2. Of those that a mesh axis runs over, the one named last changes fastest.
Arguments:
- tile_values: bfloat16 [8192, 8192], P('row', 'col'), may hold values from -1.5 to 1.5
- upper_mask: int32 [128, 128], P('row', 'col'), may hold values from 0 to 1, as said below
Outputs:
- layer_partials: float32 [8192, 32768], P('row', 'col')
The draws below stay inside these ranges and needn't reach their ends.
Inputs may be any that keep to these rules, and one draw needn't show every extreme that they name: `upper_mask`: every diagonal tile is set.
All inputs are finite; a program needn't handle non-finite values.
Results may differ from the reference program's by a relative error of at most 0.00059.
Values may be sent and summed in bfloat16 or wider, within the bound.
A program may use at most 128 MiB of HBM per device.

```python
import jax
import jax.numpy as jnp
from jax import lax

TILE = 64
BT = 16
STEPS = 2
NB = 128
N_ROW = 8
N_COL = 32


def draw_upper_mask(key, part):
    row_ids = jnp.arange(NB, dtype=jnp.int32)[:, None]
    col_ids = jnp.arange(NB, dtype=jnp.int32)[None, :]
    tile_gap = jnp.abs(row_ids - col_ids)
    cycle_gap = jnp.minimum(tile_gap, NB - tile_gap)
    band_tiles = max(NB // 6, 1)
    keep_level = jnp.maximum(700, 1000 - 300 * cycle_gap // band_tiles)
    keep_level = jnp.where(cycle_gap == 0, 1000, keep_level)
    rolled = jax.random.randint(key, (NB, NB), 0, 1000, dtype=jnp.int32)
    return (rolled < keep_level).astype(jnp.int32)


def steps_of(key, dims, shards, least, high):
    factor_of = 1.0
    for position, parts in shards:
        draws = jax.random.uniform(jax.random.fold_in(jax.random.fold_in(key, 6), position), (parts,), jnp.float32, least / len(shards), high / len(shards))
        factor_of = factor_of * jnp.repeat(jnp.exp(draws), dims[position] // parts).reshape((-1,) + (1,) * (len(dims) - 1 - position))
    return factor_of


def noise(own_key, extent, deviation, most, cuts=(), kind=jnp.bfloat16):
    array = jax.random.normal(own_key, extent, jnp.float32) * deviation
    if len(cuts) > 0:
        array = steps_of(own_key, extent, cuts, -0.22, 0.18) * array
    return jnp.clip(array, min=-most, max=most).astype(kind)


def setup_inputs(seed: int = 0) -> dict:
    key_list = jax.random.split(jax.random.key(seed), 3)
    return {
        "tile_values": noise(key_list[0], (NB * TILE, NB * TILE), 0.25, 1.5, ((0, 8), (1, 32))),
        "upper_mask": draw_upper_mask(jax.random.fold_in(key_list[2], 71), 0),
    }


def reference(tile_values, upper_mask):
    groups = N_COL // N_ROW
    height = BT * TILE
    piece_width = height // groups
    tile_index = jnp.arange(NB, dtype=jnp.int32)
    keep_tiles = (upper_mask != 0) & (tile_index[:, None] <= tile_index[None, :])
    keep_cells = jnp.repeat(jnp.repeat(keep_tiles, TILE, axis=0), TILE, axis=1)
    upper_part = jnp.where(keep_cells, tile_values, jnp.zeros_like(tile_values))
    density = (upper_part.astype(jnp.float32) + upper_part.T.astype(jnp.float32)).astype(jnp.bfloat16)
    blocks = density.reshape(N_ROW, height, N_ROW, height)

    def one_block(pair_index):
        block_row = (pair_index // N_ROW).astype(jnp.int32)
        block_col = (pair_index % N_ROW).astype(jnp.int32)
        row_slab = lax.dynamic_index_in_dim(blocks, block_row, 0, keepdims=False)
        pieces = []
        for layer_index in range(groups):
            running = jnp.zeros((height, height), jnp.float32)
            for step_index in range(STEPS):
                inner_block = ((block_row + block_col + step_index) % N_ROW).astype(jnp.int32)
                left_block = lax.dynamic_index_in_dim(row_slab, inner_block, 1, keepdims=False)
                inner_slab = lax.dynamic_index_in_dim(blocks, inner_block, 0, keepdims=False)
                right_block = lax.dynamic_index_in_dim(inner_slab, block_col, 1, keepdims=False)
                left_piece = left_block[:, layer_index * piece_width:(layer_index + 1) * piece_width]
                right_piece = right_block[layer_index * piece_width:(layer_index + 1) * piece_width, :]
                running = running + jnp.dot(left_piece, right_piece, preferred_element_type=jnp.float32)
            pieces.append(running)
        return jnp.stack(pieces)

    results = lax.map(one_block, jnp.arange(N_ROW * N_ROW, dtype=jnp.int32))
    results = results.reshape(N_ROW, N_ROW, groups, height, height)
    results = jnp.transpose(results, (0, 3, 1, 2, 4))
    return results.reshape(N_ROW * height, N_ROW * groups * height)
```

```python
import jax
import jax.numpy as jnp
from jax import lax
from jax.experimental import pallas as pl
from jax.experimental.pallas import tpu as pltpu
from jax.sharding import PartitionSpec as P

TILE = 64
GROUPS = 4
ROWS = 8
STEPS = 2
MESH = pl.DeviceIdType.MESH


def wrap(index):
    return lax.rem(index + 2 * ROWS, ROWS)


def remote(source, target, send_sem, recv_sem, row, block, group):
    return pltpu.make_async_remote_copy(
        src_ref=source,
        dst_ref=target,
        send_sem=send_sem,
        recv_sem=recv_sem,
        device_id={"row": row, "col": block * GROUPS + group},
        device_id_type=MESH,
    )


def spread_kernel(
    upper_ref,
    left_ref,
    right_ref,
    piece,
    mirror,
    mirror_send,
    mirror_recv,
    left_send,
    left_recv,
    right_send,
    right_recv,
    local_sem,
):
    row = lax.axis_index("row")
    col = lax.axis_index("col")
    block = lax.div(col, GROUPS)
    group = lax.rem(col, GROUPS)
    width = upper_ref.shape[1]
    is_upper = row < block
    is_lower = row > block
    is_diag = row == block

    def quarter(ref, g):
        return ref.at[pl.ds(g * width, width), :]

    def greet(r, b, g):
        pl.semaphore_signal(
            barrier,
            inc=1,
            device_id={"row": r, "col": b * GROUPS + g},
            device_id_type=MESH,
        )

    barrier = pltpu.get_barrier_semaphore()
    for g in range(GROUPS):

        @pl.when(is_lower | (is_diag & (group != g)))
        def _(g=g):
            greet(block, row, g)

        for s in range(STEPS):

            @pl.when((wrap(block + s) != 0) | (group != g))
            def _(g=g, s=s):
                greet(wrap(row + block + s), block, g)

    for s in range(STEPS):

        @pl.when(wrap(row + s) != 0)
        def _(s=s):
            greet(row, wrap(row + block + s), group)

    count = jnp.int32(0)
    count += jnp.where(is_upper, GROUPS, jnp.where(is_diag, GROUPS - 1, 0))
    for s in range(STEPS):
        count += jnp.where(wrap(row + s) != 0, 1, 0)
        count += jnp.where(wrap(block + s) != 0, GROUPS, GROUPS - 1)
    pl.semaphore_wait(barrier, count)

    def mirror_copy(g):
        return remote(
            quarter(upper_ref, g),
            mirror.at[group],
            mirror_send.at[g],
            mirror_recv.at[group],
            block,
            row,
            g,
        )

    def mirror_arrival(g):
        return remote(
            quarter(upper_ref, g),
            mirror.at[g],
            mirror_send.at[g],
            mirror_recv.at[g],
            block,
            row,
            g,
        )

    for g in range(GROUPS):

        @pl.when(is_upper | (is_diag & (group != g)))
        def _(g=g):
            mirror_copy(g).start()

    def left_copy(source, s):
        return remote(
            source,
            left_ref.at[s],
            left_send.at[s],
            left_recv.at[s],
            row,
            wrap(block - row - s),
            group,
        )

    def right_copy(source, s, g):
        return remote(
            quarter(source, g),
            right_ref.at[s, group],
            right_send.at[s, g],
            right_recv.at[s, group],
            wrap(row - block - s),
            block,
            g,
        )

    def right_arrival(s, g):
        return remote(
            quarter(piece, g),
            right_ref.at[s, g],
            right_send.at[s, g],
            right_recv.at[s, g],
            wrap(row - block - s),
            block,
            g,
        )

    def local_left(source, s):
        return pltpu.make_async_copy(source, left_ref.at[s], local_sem.at[0, s])

    def local_right(source, s):
        return pltpu.make_async_copy(
            quarter(source, group), right_ref.at[s, group], local_sem.at[1, s]
        )

    def send_all(source):
        for s in range(STEPS):
            stays = wrap(row + s) == 0

            @pl.when(stays)
            def _(s=s):
                local_left(source, s).start()

            @pl.when(jnp.logical_not(stays))
            def _(s=s):
                left_copy(source, s).start()

            for g in range(GROUPS):
                home = (wrap(block + s) == 0) & (group == g)

                @pl.when(home)
                def _(s=s):
                    local_right(source, s).start()

                @pl.when(jnp.logical_not(home))
                def _(s=s, g=g):
                    right_copy(source, s, g).start()

    @pl.when(is_upper)
    def _():
        send_all(upper_ref)

    for g in range(GROUPS):

        @pl.when(is_lower | (is_diag & (group != g)))
        def _(g=g):
            mirror_arrival(g).wait_recv()

        @pl.when(is_lower)
        def _(g=g):
            piece[pl.ds(g * width, width), :] = mirror[g].T

        @pl.when(is_diag & (group != g))
        def _(g=g):
            here = upper_ref[pl.ds(g * width, width), :].astype(jnp.float32)
            there = mirror[g].T.astype(jnp.float32)
            piece[pl.ds(g * width, width), :] = (here + there).astype(jnp.bfloat16)

        @pl.when(is_diag & (group == g))
        def _(g=g):
            here = upper_ref[pl.ds(g * width, width), :]
            there = here.T.astype(jnp.float32)
            piece[pl.ds(g * width, width), :] = (
                here.astype(jnp.float32) + there
            ).astype(jnp.bfloat16)

    @pl.when(jnp.logical_not(is_upper))
    def _():
        send_all(piece)

    for g in range(GROUPS):

        @pl.when(is_upper | (is_diag & (group != g)))
        def _(g=g):
            mirror_copy(g).wait_send()

    for s in range(STEPS):
        stays = wrap(row + s) == 0

        @pl.when(stays)
        def _(s=s):
            local_left(piece, s).wait()

        @pl.when(jnp.logical_not(stays))
        def _(s=s):
            left_copy(piece, s).wait()

        for g in range(GROUPS):
            home = (wrap(block + s) == 0) & (group == g)

            @pl.when(home)
            def _(s=s):
                local_right(piece, s).wait()

            @pl.when(jnp.logical_not(home))
            def _(s=s, g=g):
                right_copy(piece, s, g).wait_send()
                right_arrival(s, g).wait_recv()


def product_kernel(left_ref, right_ref, out_ref):
    out_ref[...] = jnp.dot(
        left_ref[0], right_ref[0, 0], preferred_element_type=jnp.float32
    ) + jnp.dot(left_ref[1], right_ref[1, 0], preferred_element_type=jnp.float32)


def shards(tile_values, upper_mask):
    row = lax.axis_index("row")
    col = lax.axis_index("col")
    height, width = tile_values.shape
    tiles_high = height // TILE
    tiles_wide = width // TILE
    tile_rows = row * tiles_high + jnp.arange(tiles_high, dtype=jnp.int32)
    tile_cols = col * tiles_wide + jnp.arange(tiles_wide, dtype=jnp.int32)
    keep = (upper_mask != 0) & (tile_rows[:, None] <= tile_cols[None, :])
    keep_cells = jnp.repeat(jnp.repeat(keep, TILE, axis=0), TILE, axis=1)
    upper = jnp.where(keep_cells, tile_values, jnp.zeros_like(tile_values))
    vmem = pl.BlockSpec(memory_space=pltpu.VMEM)
    dma = pltpu.SemaphoreType.DMA
    left, right = pl.pallas_call(
        spread_kernel,
        out_shape=(
            jax.ShapeDtypeStruct((STEPS, height, width), jnp.bfloat16),
            jax.ShapeDtypeStruct((STEPS, GROUPS, width, width), jnp.bfloat16),
        ),
        in_specs=[vmem],
        out_specs=(vmem, vmem),
        scratch_shapes=[
            pltpu.VMEM((height, width), jnp.bfloat16),
            pltpu.VMEM((GROUPS, width, width), jnp.bfloat16),
            dma((GROUPS,)),
            dma((GROUPS,)),
            dma((STEPS,)),
            dma((STEPS,)),
            dma((STEPS, GROUPS)),
            dma((STEPS, GROUPS)),
            dma((2, STEPS)),
        ],
        compiler_params=pltpu.CompilerParams(collective_id=0, has_side_effects=True),
    )(upper)
    return pl.pallas_call(
        product_kernel,
        grid=(GROUPS,),
        out_shape=jax.ShapeDtypeStruct((height, height), jnp.float32),
        in_specs=[
            pl.BlockSpec((STEPS, height, width), lambda g: (0, 0, 0)),
            pl.BlockSpec((STEPS, 1, width, width), lambda g: (0, g, 0, 0)),
        ],
        out_specs=pl.BlockSpec((height, width), lambda g: (0, g)),
    )(left, right)


def solution(mesh):
    in_specs = (P("row", "col"), P("row", "col"))
    out_specs = P("row", "col")
    return jax.shard_map(
        shards, mesh=mesh, in_specs=in_specs, out_specs=out_specs, check_vma=False
    )
```

```python
import jax
import jax.numpy as jnp
from jax import lax
from jax.experimental import pallas as pl
from jax.experimental.pallas import tpu as pltpu
from jax.sharding import PartitionSpec as P

TILE = 64
GROUPS = 4
ROWS = 8
STEPS = 2
MESH = pl.DeviceIdType.MESH

RELAY = (
    (
        (0, 0, 7, 5, 0, 1, 0, 2),
        (0, 0, 3, 1, 0, 0, 7, 1),
        (0, 0, 0, 4, 2, 2, 7, 4),
        (0, 0, 0, 0, 4, 4, 7, 5),
        (0, 0, 0, 0, 0, 5, 6, 3),
        (0, 0, 0, 0, 0, 0, 7, 7),
        (0, 0, 0, 0, 0, 0, 0, 7),
        (0, 0, 0, 0, 0, 0, 0, 0),
    ),
    (
        (0, 6, 5, 7, 1, 0, 2, 3),
        (0, 0, 0, 2, 7, 0, 1, 4),
        (0, 0, 0, 3, 5, 7, 0, 7),
        (0, 0, 0, 0, 3, 5, 7, 6),
        (0, 0, 0, 0, 0, 5, 7, 6),
        (0, 0, 0, 0, 0, 0, 3, 6),
        (0, 0, 0, 0, 0, 0, 0, 7),
        (0, 0, 0, 0, 0, 0, 0, 0),
    ),
)
FROM_MIRROR = (
    (0, 0, 1, 0, 0, 0, 0, 0),
    (0, 0, 0, 0, 0, 0, 0, 0),
    (1, 0, 0, 0, 1, 1, 0, 0),
    (0, 1, 1, 0, 1, 0, 0, 1),
    (0, 0, 0, 1, 0, 1, 1, 0),
    (0, 0, 0, 1, 0, 0, 1, 0),
    (0, 0, 0, 0, 0, 0, 0, 0),
    (0, 0, 0, 0, 0, 0, 0, 0),
)
FIRST = (
    (0, 0, 1, 0, 0, 0, 0, 0),
    (0, 0, 0, 0, 0, 0, 0, 0),
    (1, 0, 0, 0, 1, 1, 0, 0),
    (1, 0, 1, 0, 0, 0, 1, 0),
    (1, 0, 1, 1, 1, 0, 1, 0),
    (1, 1, 1, 0, 1, 1, 0, 1),
    (1, 1, 1, 1, 1, 1, 1, 1),
    (1, 1, 1, 1, 1, 1, 1, 1),
)


def wrap(index):
    return lax.rem(index + 2 * ROWS, ROWS)


def word_of(entries):
    return sum(entry * 8**place for place, entry in enumerate(entries))


def look(table, i, j):
    if isinstance(i, int):
        word = jnp.int32(word_of(table[i]))
    else:
        word = jnp.int32(word_of(table[0]))
        for k in range(1, ROWS):
            word = jnp.where(i == k, jnp.int32(word_of(table[k])), word)
    return lax.rem(lax.shift_right_logical(word, 3 * j), 8)


def spread_kernel(
    values_ref,
    mask_ref,
    left_ref,
    right_ref,
    piece,
    mirror,
    passing,
    held,
    relay_send,
    relay_recv,
    pass_send,
    mirror_send,
    mirror_recv,
    direct_send,
    turned_send,
    forward_send,
    left_recv,
    right_send,
    right_recv,
):
    row = lax.axis_index("row")
    col = lax.axis_index("col")
    block = lax.div(col, GROUPS)
    group = lax.rem(col, GROUPS)
    width = values_ref.shape[1]
    is_upper = row < block
    is_lower = row > block
    is_diag = row == block

    relay = [look(RELAY[p], row, block) for p in range(2)]
    back_relay = [look(RELAY[p], block, row) for p in range(2)]
    back_row = jnp.where(lax.rem(group, 2) == 0, back_relay[0], back_relay[1])
    back_row = jnp.where(is_diag, row, back_row)
    passes = {
        (a, p): (look(RELAY[p], a, block) == row) & (a < block) & (row != a)
        for a in range(ROWS)
        for p in range(2)
    }
    own_mirror = look(FROM_MIRROR, row, block) == 1
    own_first = look(FIRST, row, block)
    own_target = wrap(block - row - own_first)
    back_mirror = look(FROM_MIRROR, block, row) == 1
    back_first = look(FIRST, block, row)
    back_target = wrap(row - block - back_first)
    inner = [wrap(row + block + s) for s in range(STEPS)]
    first_here = [look(FIRST, row, inner[s]) == s for s in range(STEPS)]
    turned = [look(FROM_MIRROR, row, inner[s]) == 1 for s in range(STEPS)]

    def quarter(ref, g):
        return ref.at[pl.ds(g * width, width), :]

    def remote(source, target, send_sem, recv_sem, r, b, g):
        return pltpu.make_async_remote_copy(
            src_ref=source,
            dst_ref=target,
            send_sem=send_sem,
            recv_sem=recv_sem,
            device_id={"row": r, "col": b * GROUPS + g},
            device_id_type=MESH,
        )

    barrier = pltpu.get_barrier_semaphore()

    def greet(r, b, g):
        pl.semaphore_signal(
            barrier,
            inc=1,
            device_id={"row": r, "col": b * GROUPS + g},
            device_id_type=MESH,
        )

    count = jnp.int32(0)

    def expect(condition, amount):
        return count + jnp.where(condition, amount, 0)

    for a in range(ROWS):
        for p in range(2):

            @pl.when(passes[a, p])
            def _(a=a):
                greet(a, block, group)

            count = expect(passes[a, p], 2)
    for p in range(2):
        count = expect(is_upper & (relay[p] != row), 1)
        count = expect(is_upper & (relay[p] == row), 2)
    count = expect(is_diag, GROUPS - 1)
    for g in range(GROUPS):

        @pl.when(is_lower | (is_diag & (group != g)))
        def _(g=g):
            greet(back_row, row, g)

        for s in range(STEPS):
            home = (wrap(block + s) == 0) & (group == g)

            @pl.when(jnp.logical_not(home))
            def _(g=g, s=s):
                greet(inner[s], block, g)

            count = expect(jnp.logical_not(home), 1)
        count = expect(back_mirror, 1)
    count = expect(jnp.logical_not(own_mirror) & (own_target != block), 1)
    for s in range(STEPS):
        neighbour = wrap(block - 1 + 2 * s)
        straight = first_here[s] & jnp.logical_not(turned[s]) & (inner[s] != block)

        @pl.when(straight)
        def _(s=s):
            greet(row, inner[s], group)

        for g in range(GROUPS):

            @pl.when(first_here[s] & turned[s])
            def _(g=g, s=s):
                greet(inner[s], row, g)

        count = expect(first_here[s], 1)
        source = wrap(block + 1 - 2 * (1 - s))

        @pl.when(jnp.logical_not(first_here[s]))
        def _(source=source):
            greet(row, source, group)

    @pl.when(jnp.logical_not(is_lower))
    def _():
        lane_tile = lax.div(lax.broadcasted_iota(jnp.int32, (1, width), 1), TILE)
        tiles_wide = width // TILE
        tiles_high = values_ref.shape[0] // TILE
        for i in range(tiles_high):
            marks = jnp.zeros((1, width), jnp.int32)
            for j in range(tiles_wide):
                marks = jnp.where(lane_tile == j, mask_ref[i : i + 1, j : j + 1], marks)
            ahead = row * tiles_high + i <= col * tiles_wide + lane_tile
            keep = jnp.where((marks != 0) & ahead, 1.0, 0.0)
            keep = jnp.broadcast_to(keep, (TILE, width)) > 0.5
            rows = pl.ds(i * TILE, TILE)
            tile = values_ref[rows, :].astype(jnp.float32)
            piece[rows, :] = jnp.where(keep, tile, 0.0).astype(jnp.bfloat16)

    pl.semaphore_wait(barrier, count)

    def relay_copy(a, g):
        return remote(
            quarter(piece, g),
            passing.at[a, g],
            relay_send.at[g],
            relay_recv.at[a, g],
            relay[g % 2],
            block,
            group,
        )

    def mirror_copy(g):
        return remote(
            quarter(piece, g),
            mirror.at[group],
            mirror_send.at[g],
            mirror_recv.at[group],
            block,
            row,
            g,
        )

    def pass_copy(a, g):
        return remote(
            passing.at[a, g],
            mirror.at[group],
            pass_send.at[a, g],
            mirror_recv.at[group],
            block,
            a,
            g,
        )

    def mirror_arrival(g):
        return remote(
            quarter(piece, g),
            mirror.at[g],
            mirror_send.at[g],
            mirror_recv.at[g],
            block,
            row,
            g,
        )

    by_relay = [is_upper & (relay[p] != row) for p in range(2)]
    by_self = [is_upper & (relay[p] == row) for p in range(2)]

    for g in range(GROUPS):

        @pl.when(by_relay[g % 2])
        def _(g=g):
            relay_copy(row, g).start()

        @pl.when(by_self[g % 2] | (is_diag & (group != g)))
        def _(g=g):
            mirror_copy(g).start()

    def direct_copy(q):
        return remote(
            quarter(piece, q),
            held.at[own_first, q],
            direct_send.at[q],
            left_recv.at[own_first, q],
            row,
            own_target,
            group,
        )

    def direct_local(q):
        return pltpu.make_async_copy(
            quarter(piece, q), held.at[own_first, q], left_recv.at[own_first, q]
        )

    def turned_copy(q):
        return remote(
            quarter(piece, q),
            held.at[back_first, group],
            turned_send.at[q],
            left_recv.at[back_first, group],
            block,
            back_target,
            q,
        )

    def right_copy(s, q):
        return remote(
            quarter(piece, q),
            right_ref.at[s, group],
            right_send.at[s, q],
            right_recv.at[s, group],
            wrap(row - block - s),
            block,
            q,
        )

    def right_local(s, q):
        return pltpu.make_async_copy(
            quarter(piece, q), right_ref.at[s, group], right_recv.at[s, group]
        )

    own_far = jnp.logical_not(own_mirror) & (own_target != block)
    own_home = jnp.logical_not(own_mirror) & (own_target == block)

    def send_quarter(q):
        @pl.when(own_far)
        def _():
            direct_copy(q).start()

        @pl.when(own_home)
        def _():
            direct_local(q).start()

        @pl.when(back_mirror)
        def _():
            turned_copy(q).start()

        for s in range(STEPS):
            home = (wrap(block + s) == 0) & (group == q)

            @pl.when(home)
            def _(s=s):
                right_local(s, q).start()

            @pl.when(jnp.logical_not(home))
            def _(s=s):
                right_copy(s, q).start()

    @pl.when(is_upper)
    def _():
        for q in range(GROUPS):
            send_quarter(q)

    for a in range(ROWS):
        for g in range(GROUPS):

            @pl.when(passes[a, g % 2])
            def _(a=a, g=g):
                relay_copy(a, g).wait_recv()
                pass_copy(a, g).start()

    @pl.when(jnp.logical_not(is_upper))
    def _():
        for g in range(GROUPS):
            rows = pl.ds(g * width, width)

            @pl.when(is_lower)
            def _(g=g, rows=rows):
                mirror_arrival(g).wait_recv()
                piece[rows, :] = mirror[g].T

            @pl.when(is_diag & (group != g))
            def _(g=g, rows=rows):
                mirror_arrival(g).wait_recv()
                mirror_copy(g).wait_send()
                here = piece[rows, :].astype(jnp.float32)
                there = mirror[g].T.astype(jnp.float32)
                piece[rows, :] = (here + there).astype(jnp.bfloat16)

            @pl.when(is_diag & (group == g))
            def _(g=g, rows=rows):
                here = piece[rows, :]
                there = here.T.astype(jnp.float32)
                piece[rows, :] = (here.astype(jnp.float32) + there).astype(jnp.bfloat16)

            send_quarter(g)

    def forward_copy(s, q):
        return remote(
            held.at[s, q],
            held.at[1 - s, q],
            forward_send.at[s, q],
            left_recv.at[1 - s, q],
            row,
            wrap(block - 1 + 2 * s),
            group,
        )

    def left_arrival(s, q):
        return remote(
            quarter(piece, q),
            held.at[s, q],
            direct_send.at[q],
            left_recv.at[s, q],
            row,
            own_target,
            group,
        )

    def settle(s, q):
        rows = pl.ds(q * width, width)

        @pl.when(turned[s])
        def _():
            left_ref[s, rows, :] = held[s, q].T

        @pl.when(jnp.logical_not(turned[s]))
        def _():
            left_ref[s, rows, :] = held[s, q]

    for q in range(GROUPS):
        for s in range(STEPS):

            @pl.when(first_here[s])
            def _(s=s, q=q):
                left_arrival(s, q).wait_recv()
                forward_copy(s, q).start()

    for q in range(GROUPS):
        for s in range(STEPS):

            @pl.when(jnp.logical_not(first_here[s]))
            def _(s=s, q=q):
                left_arrival(s, q).wait_recv()

            settle(s, q)

    for g in range(GROUPS):
        for s in range(STEPS):
            remote(
                quarter(piece, g),
                right_ref.at[s, g],
                right_send.at[s, g],
                right_recv.at[s, g],
                row,
                block,
                g,
            ).wait_recv()
            home = (wrap(block + s) == 0) & (group == g)

            @pl.when(jnp.logical_not(home))
            def _(s=s, g=g):
                right_copy(s, g).wait_send()

            @pl.when(first_here[s])
            def _(s=s, g=g):
                forward_copy(s, g).wait_send()

        @pl.when(own_far)
        def _(g=g):
            direct_copy(g).wait_send()

        @pl.when(back_mirror)
        def _(g=g):
            turned_copy(g).wait_send()

        @pl.when(by_relay[g % 2])
        def _(g=g):
            relay_copy(row, g).wait_send()

        @pl.when(by_self[g % 2])
        def _(g=g):
            mirror_copy(g).wait_send()

        for a in range(ROWS):

            @pl.when(passes[a, g % 2])
            def _(a=a, g=g):
                pass_copy(a, g).wait_send()


def product_kernel(left_ref, right_ref, out_ref):
    out_ref[...] = jnp.dot(
        left_ref[0], right_ref[0, 0], preferred_element_type=jnp.float32
    ) + jnp.dot(left_ref[1], right_ref[1, 0], preferred_element_type=jnp.float32)


def shards(tile_values, upper_mask):
    height, width = tile_values.shape
    vmem = pl.BlockSpec(memory_space=pltpu.VMEM)
    dma = pltpu.SemaphoreType.DMA
    square = (width, width)
    left, right = pl.pallas_call(
        spread_kernel,
        out_shape=(
            jax.ShapeDtypeStruct((STEPS, height, width), jnp.bfloat16),
            jax.ShapeDtypeStruct((STEPS, GROUPS) + square, jnp.bfloat16),
        ),
        in_specs=[vmem, vmem],
        out_specs=(vmem, vmem),
        scratch_shapes=[
            pltpu.VMEM((height, width), jnp.bfloat16),
            pltpu.VMEM((GROUPS,) + square, jnp.bfloat16),
            pltpu.VMEM((ROWS, GROUPS) + square, jnp.bfloat16),
            pltpu.VMEM((STEPS, GROUPS) + square, jnp.bfloat16),
            dma((GROUPS,)),
            dma((ROWS, GROUPS)),
            dma((ROWS, GROUPS)),
            dma((GROUPS,)),
            dma((GROUPS,)),
            dma((GROUPS,)),
            dma((GROUPS,)),
            dma((STEPS, GROUPS)),
            dma((STEPS, GROUPS)),
            dma((STEPS, GROUPS)),
            dma((STEPS, GROUPS)),
        ],
        compiler_params=pltpu.CompilerParams(collective_id=0, has_side_effects=True),
    )(tile_values, upper_mask)
    return pl.pallas_call(
        product_kernel,
        grid=(GROUPS,),
        out_shape=jax.ShapeDtypeStruct((height, height), jnp.float32),
        in_specs=[
            pl.BlockSpec((STEPS, height, width), lambda g: (0, 0, 0)),
            pl.BlockSpec((STEPS, 1, width, width), lambda g: (0, g, 0, 0)),
        ],
        out_specs=pl.BlockSpec((height, width), lambda g: (0, g)),
    )(left, right)


def solution(mesh):
    in_specs = (P("row", "col"), P("row", "col"))
    out_specs = P("row", "col")
    return jax.shard_map(
        shards, mesh=mesh, in_specs=in_specs, out_specs=out_specs, check_vma=False
    )
```

```python
import jax
import jax.numpy as jnp
from jax import lax
from jax.experimental import pallas as pl
from jax.experimental.pallas import tpu as pltpu
from jax.sharding import PartitionSpec as P

TILE = 64
GROUPS = 4
ROWS = 8
STEPS = 2
MESH = pl.DeviceIdType.MESH

RELAY = (
    (
        (0, 6, 7, 4, 5, 2, 7, 1),
        (0, 0, 7, 1, 3, 5, 7, 3),
        (0, 0, 0, 0, 7, 4, 0, 4),
        (0, 0, 0, 0, 5, 2, 5, 1),
        (0, 0, 0, 0, 0, 2, 2, 0),
        (0, 0, 0, 0, 0, 0, 3, 4),
        (0, 0, 0, 0, 0, 0, 0, 4),
        (0, 0, 0, 0, 0, 0, 0, 0),
    ),
    (
        (0, 0, 1, 4, 2, 0, 2, 3),
        (0, 0, 4, 7, 0, 2, 1, 7),
        (0, 0, 0, 6, 2, 3, 5, 3),
        (0, 0, 0, 0, 4, 4, 1, 6),
        (0, 0, 0, 0, 0, 4, 7, 6),
        (0, 0, 0, 0, 0, 0, 4, 7),
        (0, 0, 0, 0, 0, 0, 0, 7),
        (0, 0, 0, 0, 0, 0, 0, 0),
    ),
    (
        (0, 0, 2, 3, 3, 7, 5, 1),
        (0, 0, 2, 2, 0, 6, 6, 0),
        (0, 0, 0, 5, 7, 1, 0, 6),
        (0, 0, 0, 0, 6, 3, 7, 5),
        (0, 0, 0, 0, 0, 3, 3, 7),
        (0, 0, 0, 0, 0, 0, 4, 2),
        (0, 0, 0, 0, 0, 0, 0, 4),
        (0, 0, 0, 0, 0, 0, 0, 0),
    ),
    (
        (0, 2, 6, 1, 4, 2, 1, 6),
        (0, 0, 3, 5, 6, 0, 6, 4),
        (0, 0, 0, 3, 2, 4, 4, 5),
        (0, 0, 0, 0, 3, 7, 0, 1),
        (0, 0, 0, 0, 0, 5, 6, 0),
        (0, 0, 0, 0, 0, 0, 3, 5),
        (0, 0, 0, 0, 0, 0, 0, 6),
        (0, 0, 0, 0, 0, 0, 0, 0),
    ),
)
FROM_MIRROR = (
    (0, 0, 0, 0, 0, 0, 0, 0),
    (0, 0, 0, 0, 0, 0, 0, 1),
    (0, 1, 0, 0, 1, 1, 0, 1),
    (0, 1, 1, 0, 1, 0, 0, 1),
    (1, 0, 1, 1, 0, 1, 1, 0),
    (0, 0, 0, 1, 1, 0, 0, 1),
    (1, 0, 0, 0, 0, 0, 0, 0),
    (0, 0, 0, 0, 0, 0, 0, 0),
)
FIRST = (
    (0, 0, 0, 0, 0, 0, 0, 0),
    (0, 0, 0, 0, 0, 0, 0, 0),
    (0, 1, 0, 0, 1, 1, 0, 0),
    (0, 0, 1, 0, 1, 0, 1, 0),
    (1, 1, 0, 0, 1, 0, 1, 0),
    (1, 1, 1, 0, 0, 1, 1, 0),
    (1, 1, 1, 1, 1, 1, 1, 1),
    (1, 1, 1, 1, 1, 1, 1, 1),
)


def wrap(index):
    return lax.rem(index + 2 * ROWS, ROWS)


def word_of(entries):
    return sum(entry * 8**place for place, entry in enumerate(entries))


def look(table, i, j):
    if isinstance(i, int):
        word = jnp.int32(word_of(table[i]))
    else:
        word = jnp.int32(word_of(table[0]))
        for k in range(1, ROWS):
            word = jnp.where(i == k, jnp.int32(word_of(table[k])), word)
    return lax.rem(lax.shift_right_logical(word, 3 * j), 8)


def spread_kernel(
    values_ref,
    mask_ref,
    left_ref,
    right_ref,
    piece,
    mirror,
    passing,
    held,
    relay_send,
    relay_recv,
    pass_send,
    mirror_send,
    mirror_recv,
    direct_send,
    turned_send,
    forward_send,
    left_recv,
    right_send,
    right_recv,
):
    row = lax.axis_index("row")
    col = lax.axis_index("col")
    block = lax.div(col, GROUPS)
    group = lax.rem(col, GROUPS)
    width = values_ref.shape[1]
    is_upper = row < block
    is_lower = row > block
    is_diag = row == block

    relay = [look(RELAY[g], row, block) for g in range(GROUPS)]
    back_row = row
    for g in range(GROUPS):
        back_row = jnp.where(
            is_lower & (group == g), look(RELAY[g], block, row), back_row
        )
    passes = {
        (a, g): (look(RELAY[g], a, block) == row) & (a < block) & (row != a)
        for a in range(ROWS)
        for g in range(GROUPS)
    }
    own_mirror = look(FROM_MIRROR, row, block) == 1
    own_first = look(FIRST, row, block)
    own_target = wrap(block - row - own_first)
    back_mirror = look(FROM_MIRROR, block, row) == 1
    back_first = look(FIRST, block, row)
    back_target = wrap(row - block - back_first)
    inner = [wrap(row + block + s) for s in range(STEPS)]
    first_here = [look(FIRST, row, inner[s]) == s for s in range(STEPS)]
    turned = [look(FROM_MIRROR, row, inner[s]) == 1 for s in range(STEPS)]

    def quarter(ref, g):
        return ref.at[pl.ds(g * width, width), :]

    def right_block(s, g):
        place = g * width if isinstance(g, int) else pl.multiple_of(g * width, width)
        return right_ref.at[pl.ds(s * width, width), pl.ds(place, width)]

    def remote(source, target, send_sem, recv_sem, r, b, g):
        return pltpu.make_async_remote_copy(
            src_ref=source,
            dst_ref=target,
            send_sem=send_sem,
            recv_sem=recv_sem,
            device_id={"row": r, "col": b * GROUPS + g},
            device_id_type=MESH,
        )

    barrier = pltpu.get_barrier_semaphore()

    def greet(r, b, g):
        pl.semaphore_signal(
            barrier,
            inc=1,
            device_id={"row": r, "col": b * GROUPS + g},
            device_id_type=MESH,
        )

    count = jnp.int32(0)

    def expect(condition, amount):
        return count + jnp.where(condition, amount, 0)

    for a in range(ROWS):
        for g in range(GROUPS):

            @pl.when(passes[a, g])
            def _(a=a):
                greet(a, block, group)

            count = expect(passes[a, g], 1)
    count = expect(is_upper, GROUPS)
    count = expect(is_diag, GROUPS - 1)
    for g in range(GROUPS):

        @pl.when(is_lower | (is_diag & (group != g)))
        def _(g=g):
            greet(back_row, row, g)

        for s in range(STEPS):
            home = (wrap(block + s) == 0) & (group == g)

            @pl.when(jnp.logical_not(home))
            def _(g=g, s=s):
                greet(inner[s], block, g)

            count = expect(jnp.logical_not(home), 1)
        count = expect(back_mirror, 1)
    count = expect(jnp.logical_not(own_mirror) & (own_target != block), 1)
    for s in range(STEPS):
        neighbour = wrap(block - 1 + 2 * s)
        straight = first_here[s] & jnp.logical_not(turned[s]) & (inner[s] != block)

        @pl.when(straight)
        def _(s=s):
            greet(row, inner[s], group)

        for g in range(GROUPS):

            @pl.when(first_here[s] & turned[s])
            def _(g=g, s=s):
                greet(inner[s], row, g)

        count = expect(first_here[s], 1)
        source = wrap(block + 1 - 2 * (1 - s))

        @pl.when(jnp.logical_not(first_here[s]))
        def _(source=source):
            greet(row, source, group)

    @pl.when(jnp.logical_not(is_lower))
    def _():
        lane_tile = lax.div(lax.broadcasted_iota(jnp.int32, (1, width), 1), TILE)
        tiles_wide = width // TILE
        tiles_high = values_ref.shape[0] // TILE
        for i in range(tiles_high):
            marks = jnp.zeros((1, width), jnp.int32)
            for j in range(tiles_wide):
                marks = jnp.where(lane_tile == j, mask_ref[j : j + 1, i : i + 1], marks)
            ahead = row * tiles_high + i <= col * tiles_wide + lane_tile
            keep = jnp.where((marks != 0) & ahead, 1.0, 0.0)
            keep = jnp.broadcast_to(keep, (TILE, width)) > 0.5
            rows = pl.ds(i * TILE, TILE)
            tile = values_ref[rows, :].astype(jnp.float32)
            piece[rows, :] = jnp.where(keep, tile, 0.0).astype(jnp.bfloat16)

    pl.semaphore_wait(barrier, count)

    def relay_copy(a, g):
        return remote(
            quarter(piece, g),
            passing.at[a, g],
            relay_send.at[g],
            relay_recv.at[a, g],
            relay[g],
            block,
            group,
        )

    def mirror_copy(g):
        return remote(
            quarter(piece, g),
            mirror.at[group],
            mirror_send.at[g],
            mirror_recv.at[group],
            block,
            row,
            g,
        )

    def pass_copy(a, g):
        return remote(
            passing.at[a, g],
            mirror.at[group],
            pass_send.at[a, g],
            mirror_recv.at[group],
            block,
            a,
            g,
        )

    def mirror_arrival(g):
        return remote(
            quarter(piece, g),
            mirror.at[g],
            mirror_send.at[g],
            mirror_recv.at[g],
            block,
            row,
            g,
        )

    by_relay = [is_upper & (relay[g] != row) for g in range(GROUPS)]
    by_self = [is_upper & (relay[g] == row) for g in range(GROUPS)]

    for g in range(GROUPS):

        @pl.when(by_relay[g])
        def _(g=g):
            relay_copy(row, g).start()

        @pl.when(by_self[g] | (is_diag & (group != g)))
        def _(g=g):
            mirror_copy(g).start()

    def direct_copy(q):
        return remote(
            quarter(piece, q),
            held.at[own_first, q],
            direct_send.at[q],
            left_recv.at[own_first, q],
            row,
            own_target,
            group,
        )

    def direct_local(q):
        return pltpu.make_async_copy(
            quarter(piece, q), held.at[own_first, q], left_recv.at[own_first, q]
        )

    def turned_copy(q):
        return remote(
            quarter(piece, q),
            held.at[back_first, group],
            turned_send.at[q],
            left_recv.at[back_first, group],
            block,
            back_target,
            q,
        )

    def right_copy(s, q):
        return remote(
            quarter(piece, q),
            right_block(s, group),
            right_send.at[s, q],
            right_recv.at[s, group],
            wrap(row - block - s),
            block,
            q,
        )

    def right_local(s, q):
        return pltpu.make_async_copy(
            quarter(piece, q), right_block(s, group), right_recv.at[s, group]
        )

    own_far = jnp.logical_not(own_mirror) & (own_target != block)
    own_home = jnp.logical_not(own_mirror) & (own_target == block)

    def send_left(q):
        @pl.when(own_far)
        def _():
            direct_copy(q).start()

        @pl.when(own_home)
        def _():
            direct_local(q).start()

        @pl.when(back_mirror)
        def _():
            turned_copy(q).start()

    def send_right(q):
        for s in range(STEPS):
            home = (wrap(block + s) == 0) & (group == q)

            @pl.when(home)
            def _(s=s):
                right_local(s, q).start()

            @pl.when(jnp.logical_not(home))
            def _(s=s):
                right_copy(s, q).start()

    for a in range(ROWS):
        for g in range(GROUPS):

            @pl.when(passes[a, g])
            def _(a=a, g=g):
                relay_copy(a, g).wait_recv()
                pass_copy(a, g).start()

    @pl.when(is_upper)
    def _():
        for q in range(GROUPS):
            send_left(q)
        for q in range(GROUPS):
            send_right(q)

    @pl.when(jnp.logical_not(is_upper))
    def _():
        for g in range(GROUPS):
            rows = pl.ds(g * width, width)

            @pl.when(is_lower)
            def _(g=g, rows=rows):
                mirror_arrival(g).wait_recv()
                piece[rows, :] = mirror[g].T

            @pl.when(is_diag & (group != g))
            def _(g=g, rows=rows):
                mirror_arrival(g).wait_recv()
                mirror_copy(g).wait_send()
                here = piece[rows, :].astype(jnp.float32)
                there = mirror[g].T.astype(jnp.float32)
                piece[rows, :] = (here + there).astype(jnp.bfloat16)

            @pl.when(is_diag & (group == g))
            def _(g=g, rows=rows):
                here = piece[rows, :]
                there = here.T.astype(jnp.float32)
                piece[rows, :] = (here.astype(jnp.float32) + there).astype(jnp.bfloat16)

            send_left(g)
        for g in range(GROUPS):
            send_right(g)

    def forward_copy(s, q):
        return remote(
            held.at[s, q],
            held.at[1 - s, q],
            forward_send.at[s, q],
            left_recv.at[1 - s, q],
            row,
            wrap(block - 1 + 2 * s),
            group,
        )

    def left_arrival(s, q):
        return remote(
            quarter(piece, q),
            held.at[s, q],
            direct_send.at[q],
            left_recv.at[s, q],
            row,
            own_target,
            group,
        )

    def settle(s, q):
        rows = pl.ds(q * width, width)

        @pl.when(turned[s])
        def _():
            left_ref[rows, s * width : (s + 1) * width] = held[s, q].T

        @pl.when(jnp.logical_not(turned[s]))
        def _():
            left_ref[rows, s * width : (s + 1) * width] = held[s, q]

    for q in range(GROUPS):
        for s in range(STEPS):

            @pl.when(first_here[s])
            def _(s=s, q=q):
                left_arrival(s, q).wait_recv()
                forward_copy(s, q).start()

    for q in range(GROUPS):
        for s in range(STEPS):

            @pl.when(jnp.logical_not(first_here[s]))
            def _(s=s, q=q):
                left_arrival(s, q).wait_recv()

            settle(s, q)

    for g in range(GROUPS):
        for s in range(STEPS):
            remote(
                quarter(piece, g),
                right_block(s, g),
                right_send.at[s, g],
                right_recv.at[s, g],
                row,
                block,
                g,
            ).wait_recv()
            home = (wrap(block + s) == 0) & (group == g)

            @pl.when(jnp.logical_not(home))
            def _(s=s, g=g):
                right_copy(s, g).wait_send()

            @pl.when(first_here[s])
            def _(s=s, g=g):
                forward_copy(s, g).wait_send()

        @pl.when(own_far)
        def _(g=g):
            direct_copy(g).wait_send()

        @pl.when(back_mirror)
        def _(g=g):
            turned_copy(g).wait_send()

        for a in range(ROWS):

            @pl.when(passes[a, g])
            def _(a=a, g=g):
                pass_copy(a, g).wait_send()

    for g in range(GROUPS):

        @pl.when(by_relay[g])
        def _(g=g):
            relay_copy(row, g).wait_send()

        @pl.when(by_self[g])
        def _(g=g):
            mirror_copy(g).wait_send()


def shards(tile_values, upper_mask):
    height, width = tile_values.shape
    vmem = pl.BlockSpec(memory_space=pltpu.VMEM)
    dma = pltpu.SemaphoreType.DMA
    square = (width, width)
    left, right = pl.pallas_call(
        spread_kernel,
        out_shape=(
            jax.ShapeDtypeStruct((height, STEPS * width), jnp.bfloat16),
            jax.ShapeDtypeStruct((STEPS * width, height), jnp.bfloat16),
        ),
        in_specs=[vmem, vmem],
        out_specs=(vmem, vmem),
        scratch_shapes=[
            pltpu.VMEM((height, width), jnp.bfloat16),
            pltpu.VMEM((GROUPS,) + square, jnp.bfloat16),
            pltpu.VMEM((ROWS, GROUPS) + square, jnp.bfloat16),
            pltpu.VMEM((STEPS, GROUPS) + square, jnp.bfloat16),
            dma((GROUPS,)),
            dma((ROWS, GROUPS)),
            dma((ROWS, GROUPS)),
            dma((GROUPS,)),
            dma((GROUPS,)),
            dma((GROUPS,)),
            dma((GROUPS,)),
            dma((STEPS, GROUPS)),
            dma((STEPS, GROUPS)),
            dma((STEPS, GROUPS)),
            dma((STEPS, GROUPS)),
        ],
        compiler_params=pltpu.CompilerParams(collective_id=0, has_side_effects=True),
    )(tile_values, upper_mask.T)
    return jnp.dot(left, right, preferred_element_type=jnp.float32)


def solution(mesh):
    in_specs = (P("row", "col"), P("row", "col"))
    out_specs = P("row", "col")
    return jax.shard_map(
        shards, mesh=mesh, in_specs=in_specs, out_specs=out_specs, check_vma=False
    )
```

```python
import jax
import jax.numpy as jnp
from jax import lax
from jax.experimental import pallas as pl
from jax.experimental.pallas import tpu as pltpu
from jax.sharding import PartitionSpec as P

TILE = 64
GROUPS = 4
ROWS = 8
STEPS = 2
MESH = pl.DeviceIdType.MESH

RELAY = (
    (
        (0, 6, 7, 4, 5, 2, 7, 1),
        (0, 0, 7, 1, 3, 5, 7, 3),
        (0, 0, 0, 0, 7, 4, 0, 4),
        (0, 0, 0, 0, 5, 2, 5, 1),
        (0, 0, 0, 0, 0, 2, 2, 0),
        (0, 0, 0, 0, 0, 0, 3, 4),
        (0, 0, 0, 0, 0, 0, 0, 4),
        (0, 0, 0, 0, 0, 0, 0, 0),
    ),
    (
        (0, 0, 1, 4, 2, 0, 2, 3),
        (0, 0, 4, 7, 0, 2, 1, 7),
        (0, 0, 0, 6, 2, 3, 5, 3),
        (0, 0, 0, 0, 4, 4, 1, 6),
        (0, 0, 0, 0, 0, 4, 7, 6),
        (0, 0, 0, 0, 0, 0, 4, 7),
        (0, 0, 0, 0, 0, 0, 0, 7),
        (0, 0, 0, 0, 0, 0, 0, 0),
    ),
    (
        (0, 0, 2, 3, 3, 7, 5, 1),
        (0, 0, 2, 2, 0, 6, 6, 0),
        (0, 0, 0, 5, 7, 1, 0, 6),
        (0, 0, 0, 0, 6, 3, 7, 5),
        (0, 0, 0, 0, 0, 3, 3, 7),
        (0, 0, 0, 0, 0, 0, 4, 2),
        (0, 0, 0, 0, 0, 0, 0, 4),
        (0, 0, 0, 0, 0, 0, 0, 0),
    ),
    (
        (0, 2, 6, 1, 4, 2, 1, 6),
        (0, 0, 3, 5, 6, 0, 6, 4),
        (0, 0, 0, 3, 2, 4, 4, 5),
        (0, 0, 0, 0, 3, 7, 0, 1),
        (0, 0, 0, 0, 0, 5, 6, 0),
        (0, 0, 0, 0, 0, 0, 3, 5),
        (0, 0, 0, 0, 0, 0, 0, 6),
        (0, 0, 0, 0, 0, 0, 0, 0),
    ),
)
FROM_MIRROR = (
    (0, 0, 0, 0, 0, 0, 0, 0),
    (0, 0, 0, 0, 0, 0, 0, 1),
    (0, 1, 0, 0, 1, 1, 0, 1),
    (0, 1, 1, 0, 1, 0, 0, 1),
    (1, 0, 1, 1, 0, 1, 1, 0),
    (0, 0, 0, 1, 1, 0, 0, 1),
    (1, 0, 0, 0, 0, 0, 0, 0),
    (0, 0, 0, 0, 0, 0, 0, 0),
)
FIRST = (
    (0, 0, 0, 0, 0, 0, 0, 0),
    (0, 0, 0, 0, 0, 0, 0, 0),
    (0, 1, 0, 0, 1, 1, 0, 0),
    (0, 0, 1, 0, 1, 0, 1, 0),
    (1, 1, 0, 0, 1, 0, 1, 0),
    (1, 1, 1, 0, 0, 1, 1, 0),
    (1, 1, 1, 1, 1, 1, 1, 1),
    (1, 1, 1, 1, 1, 1, 1, 1),
)


def wrap(index):
    return lax.rem(index + 2 * ROWS, ROWS)


def word_of(entries):
    return sum(entry * 8**place for place, entry in enumerate(entries))


def look(table, i, j):
    if isinstance(i, int):
        word = jnp.int32(word_of(table[i]))
    else:
        word = jnp.int32(word_of(table[0]))
        for k in range(1, ROWS):
            word = jnp.where(i == k, jnp.int32(word_of(table[k])), word)
    return lax.rem(lax.shift_right_logical(word, 3 * j), 8)


def spread_kernel(
    values_ref,
    mask_ref,
    left_ref,
    right_ref,
    piece,
    mirror,
    passing,
    held,
    relay_send,
    relay_recv,
    pass_send,
    mirror_send,
    mirror_recv,
    direct_send,
    turned_send,
    forward_send,
    left_recv,
    right_send,
    right_recv,
):
    row = lax.axis_index("row")
    col = lax.axis_index("col")
    block = lax.div(col, GROUPS)
    group = lax.rem(col, GROUPS)
    width = values_ref.shape[1]
    is_upper = row < block
    is_lower = row > block
    is_diag = row == block

    relay = [look(RELAY[g], row, block) for g in range(GROUPS)]
    back_row = row
    for g in range(GROUPS):
        back_row = jnp.where(
            is_lower & (group == g), look(RELAY[g], block, row), back_row
        )
    passes = {
        (a, g): (look(RELAY[g], a, block) == row) & (a < block) & (row != a)
        for a in range(ROWS)
        for g in range(GROUPS)
    }
    own_mirror = look(FROM_MIRROR, row, block) == 1
    own_first = look(FIRST, row, block)
    own_target = wrap(block - row - own_first)
    back_mirror = look(FROM_MIRROR, block, row) == 1
    back_first = look(FIRST, block, row)
    back_target = wrap(row - block - back_first)
    inner = [wrap(row + block + s) for s in range(STEPS)]
    first_here = [look(FIRST, row, inner[s]) == s for s in range(STEPS)]
    turned = [look(FROM_MIRROR, row, inner[s]) == 1 for s in range(STEPS)]

    def quarter(ref, g):
        return ref.at[pl.ds(g * width, width), :]

    def right_block(s, g):
        place = g * width if isinstance(g, int) else pl.multiple_of(g * width, width)
        return right_ref.at[pl.ds(s * width, width), pl.ds(place, width)]

    def remote(source, target, send_sem, recv_sem, r, b, g):
        return pltpu.make_async_remote_copy(
            src_ref=source,
            dst_ref=target,
            send_sem=send_sem,
            recv_sem=recv_sem,
            device_id={"row": r, "col": b * GROUPS + g},
            device_id_type=MESH,
        )

    barrier = pltpu.get_barrier_semaphore()

    def greet(r, b, g):
        pl.semaphore_signal(
            barrier,
            inc=1,
            device_id={"row": r, "col": b * GROUPS + g},
            device_id_type=MESH,
        )

    count = jnp.int32(0)

    def expect(condition, amount):
        return count + jnp.where(condition, amount, 0)

    for a in range(ROWS):
        for g in range(GROUPS):

            @pl.when(passes[a, g])
            def _(a=a):
                greet(a, block, group)

            count = expect(passes[a, g], 1)
    count = expect(is_upper, GROUPS)
    count = expect(is_diag, GROUPS - 1)
    for g in range(GROUPS):

        @pl.when(is_lower | (is_diag & (group != g)))
        def _(g=g):
            greet(back_row, row, g)

        for s in range(STEPS):
            home = (wrap(block + s) == 0) & (group == g)

            @pl.when(jnp.logical_not(home))
            def _(g=g, s=s):
                greet(inner[s], block, g)

            count = expect(jnp.logical_not(home), 1)
        count = expect(back_mirror, 1)
    count = expect(jnp.logical_not(own_mirror) & (own_target != block), 1)
    for s in range(STEPS):
        neighbour = wrap(block - 1 + 2 * s)
        straight = first_here[s] & jnp.logical_not(turned[s]) & (inner[s] != block)

        @pl.when(straight)
        def _(s=s):
            greet(row, inner[s], group)

        for g in range(GROUPS):

            @pl.when(first_here[s] & turned[s])
            def _(g=g, s=s):
                greet(inner[s], row, g)

        count = expect(first_here[s], 1)
        source = wrap(block + 1 - 2 * (1 - s))

        @pl.when(jnp.logical_not(first_here[s]))
        def _(source=source):
            greet(row, source, group)

    @pl.when(jnp.logical_not(is_lower))
    def _():
        lane_tile = lax.div(lax.broadcasted_iota(jnp.int32, (1, width), 1), TILE)
        tiles_wide = width // TILE
        tiles_high = values_ref.shape[0] // TILE
        for i in range(tiles_high):
            marks = jnp.zeros((1, width), jnp.int32)
            for j in range(tiles_wide):
                marks = jnp.where(lane_tile == j, mask_ref[j : j + 1, i : i + 1], marks)
            ahead = row * tiles_high + i <= col * tiles_wide + lane_tile
            keep = jnp.where((marks != 0) & ahead, 1.0, 0.0)
            keep = jnp.broadcast_to(keep, (TILE, width)) > 0.5
            rows = pl.ds(i * TILE, TILE)
            tile = values_ref[rows, :].astype(jnp.float32)
            piece[rows, :] = jnp.where(keep, tile, 0.0).astype(jnp.bfloat16)

    pl.semaphore_wait(barrier, count)

    def relay_copy(a, g):
        return remote(
            quarter(piece, g),
            passing.at[a, g],
            relay_send.at[g],
            relay_recv.at[a, g],
            relay[g],
            block,
            group,
        )

    def mirror_copy(g):
        return remote(
            quarter(piece, g),
            mirror.at[group],
            mirror_send.at[g],
            mirror_recv.at[group],
            block,
            row,
            g,
        )

    def pass_copy(a, g):
        return remote(
            passing.at[a, g],
            mirror.at[group],
            pass_send.at[a, g],
            mirror_recv.at[group],
            block,
            a,
            g,
        )

    def mirror_arrival(g):
        return remote(
            quarter(piece, g),
            mirror.at[g],
            mirror_send.at[g],
            mirror_recv.at[g],
            block,
            row,
            g,
        )

    by_relay = [is_upper & (relay[g] != row) for g in range(GROUPS)]
    by_self = [is_upper & (relay[g] == row) for g in range(GROUPS)]

    for g in range(GROUPS):

        @pl.when(by_relay[g])
        def _(g=g):
            relay_copy(row, g).start()

        @pl.when(by_self[g] | (is_diag & (group != g)))
        def _(g=g):
            mirror_copy(g).start()

    def direct_copy(q):
        return remote(
            quarter(piece, q),
            held.at[own_first, q],
            direct_send.at[q],
            left_recv.at[own_first, q],
            row,
            own_target,
            group,
        )

    def direct_local(q):
        return pltpu.make_async_copy(
            quarter(piece, q), held.at[own_first, q], left_recv.at[own_first, q]
        )

    def turned_copy(q):
        return remote(
            quarter(piece, q),
            held.at[back_first, group],
            turned_send.at[q],
            left_recv.at[back_first, group],
            block,
            back_target,
            q,
        )

    def right_copy(s, q):
        return remote(
            quarter(piece, q),
            right_block(s, group),
            right_send.at[s, q],
            right_recv.at[s, group],
            wrap(row - block - s),
            block,
            q,
        )

    def right_local(s, q):
        return pltpu.make_async_copy(
            quarter(piece, q), right_block(s, group), right_recv.at[s, group]
        )

    own_far = jnp.logical_not(own_mirror) & (own_target != block)
    own_home = jnp.logical_not(own_mirror) & (own_target == block)

    def send_left(q):
        @pl.when(own_far)
        def _():
            direct_copy(q).start()

        @pl.when(own_home)
        def _():
            direct_local(q).start()

        @pl.when(back_mirror)
        def _():
            turned_copy(q).start()

    def send_right(q):
        for s in range(STEPS):
            home = (wrap(block + s) == 0) & (group == q)

            @pl.when(home)
            def _(s=s):
                right_local(s, q).start()

            @pl.when(jnp.logical_not(home))
            def _(s=s):
                right_copy(s, q).start()

    for g in range(GROUPS):
        for a in range(ROWS):

            @pl.when(passes[a, g])
            def _(a=a, g=g):
                relay_copy(a, g).wait_recv()
                pass_copy(a, g).start()

    @pl.when(is_upper)
    def _():
        for q in range(GROUPS):
            send_left(q)
        for q in range(GROUPS):
            send_right(q)

    @pl.when(jnp.logical_not(is_upper))
    def _():
        for g in range(GROUPS):
            rows = pl.ds(g * width, width)

            @pl.when(is_lower)
            def _(g=g, rows=rows):
                mirror_arrival(g).wait_recv()
                piece[rows, :] = mirror[g].T

            @pl.when(is_diag & (group != g))
            def _(g=g, rows=rows):
                mirror_arrival(g).wait_recv()
                mirror_copy(g).wait_send()
                here = piece[rows, :].astype(jnp.float32)
                there = mirror[g].T.astype(jnp.float32)
                piece[rows, :] = (here + there).astype(jnp.bfloat16)

            @pl.when(is_diag & (group == g))
            def _(g=g, rows=rows):
                here = piece[rows, :]
                there = here.T.astype(jnp.float32)
                piece[rows, :] = (here.astype(jnp.float32) + there).astype(jnp.bfloat16)

            send_left(g)
        for g in range(GROUPS):
            send_right(g)

    def forward_copy(s, q):
        return remote(
            held.at[s, q],
            held.at[1 - s, q],
            forward_send.at[s, q],
            left_recv.at[1 - s, q],
            row,
            wrap(block - 1 + 2 * s),
            group,
        )

    def left_arrival(s, q):
        return remote(
            quarter(piece, q),
            held.at[s, q],
            direct_send.at[q],
            left_recv.at[s, q],
            row,
            own_target,
            group,
        )

    def settle(s, q):
        rows = pl.ds(q * width, width)

        @pl.when(turned[s])
        def _():
            left_ref[rows, s * width : (s + 1) * width] = held[s, q].T

        @pl.when(jnp.logical_not(turned[s]))
        def _():
            left_ref[rows, s * width : (s + 1) * width] = held[s, q]

    for q in range(GROUPS):
        for s in range(STEPS):

            @pl.when(first_here[s])
            def _(s=s, q=q):
                left_arrival(s, q).wait_recv()
                forward_copy(s, q).start()

    for q in range(GROUPS):
        for s in range(STEPS):

            @pl.when(jnp.logical_not(first_here[s]))
            def _(s=s, q=q):
                left_arrival(s, q).wait_recv()

            settle(s, q)

    for g in range(GROUPS):
        for s in range(STEPS):
            remote(
                quarter(piece, g),
                right_block(s, g),
                right_send.at[s, g],
                right_recv.at[s, g],
                row,
                block,
                g,
            ).wait_recv()
            home = (wrap(block + s) == 0) & (group == g)

            @pl.when(jnp.logical_not(home))
            def _(s=s, g=g):
                right_copy(s, g).wait_send()

            @pl.when(first_here[s])
            def _(s=s, g=g):
                forward_copy(s, g).wait_send()

        @pl.when(own_far)
        def _(g=g):
            direct_copy(g).wait_send()

        @pl.when(back_mirror)
        def _(g=g):
            turned_copy(g).wait_send()

        for a in range(ROWS):

            @pl.when(passes[a, g])
            def _(a=a, g=g):
                pass_copy(a, g).wait_send()

    for g in range(GROUPS):

        @pl.when(by_relay[g])
        def _(g=g):
            relay_copy(row, g).wait_send()

        @pl.when(by_self[g])
        def _(g=g):
            mirror_copy(g).wait_send()


def shards(tile_values, upper_mask):
    height, width = tile_values.shape
    vmem = pl.BlockSpec(memory_space=pltpu.VMEM)
    dma = pltpu.SemaphoreType.DMA
    square = (width, width)
    left, right = pl.pallas_call(
        spread_kernel,
        out_shape=(
            jax.ShapeDtypeStruct((height, STEPS * width), jnp.bfloat16),
            jax.ShapeDtypeStruct((STEPS * width, height), jnp.bfloat16),
        ),
        in_specs=[vmem, vmem],
        out_specs=(vmem, vmem),
        scratch_shapes=[
            pltpu.VMEM((height, width), jnp.bfloat16),
            pltpu.VMEM((GROUPS,) + square, jnp.bfloat16),
            pltpu.VMEM((ROWS, GROUPS) + square, jnp.bfloat16),
            pltpu.VMEM((STEPS, GROUPS) + square, jnp.bfloat16),
            dma((GROUPS,)),
            dma((ROWS, GROUPS)),
            dma((ROWS, GROUPS)),
            dma((GROUPS,)),
            dma((GROUPS,)),
            dma((GROUPS,)),
            dma((GROUPS,)),
            dma((STEPS, GROUPS)),
            dma((STEPS, GROUPS)),
            dma((STEPS, GROUPS)),
            dma((STEPS, GROUPS)),
        ],
        compiler_params=pltpu.CompilerParams(collective_id=0, has_side_effects=True),
    )(tile_values, upper_mask.T)
    return jnp.dot(left, right, preferred_element_type=jnp.float32)


def solution(mesh):
    in_specs = (P("row", "col"), P("row", "col"))
    out_specs = P("row", "col")
    return jax.shard_map(
        shards, mesh=mesh, in_specs=in_specs, out_specs=out_specs, check_vma=False
    )
```
